128 devices in a mesh: ctx: 32 (over z_hi, x, y), kv: 4 (over z_lo, core).
Axes of the slice: x: 4, y: 4, z: 4 (z_hi: 2, z_lo: 2; z = z_hi * 2 + z_lo), core: 2. Of those that a mesh axis runs over, the one named last changes fastest.
Arguments:
- queries: bfloat16 [12288, 64, 128], P('ctx', 'kv'), may hold values from -128 to 128
- key_heads: bfloat16 [12288, 8, 128], P('ctx', 'kv'), may hold values from -6 to 6
- value_heads: bfloat16 [12288, 8, 128], P('ctx', 'kv'), may hold values from -6 to 6
- grad_out: bfloat16 [12288, 64, 128], P('ctx', 'kv'), may hold values from -6 to 6
- transforms: float32 [32, 128, 128], P('ctx'), may hold values from -1.2 to 1.2
- window: int32 [8], P('kv'), may hold values from 1 to 4, as said below
- first_block: int32 [1], replicated, may hold values from 0 to 31
Outputs:
- query_grad: bfloat16 [12288, 64, 128], P('ctx', 'kv')
- key_grad: bfloat16 [12288, 8, 128], P('ctx', 'kv')
- value_grad: bfloat16 [12288, 8, 128], P('ctx', 'kv')
- turn_grad: float32 [32, 128, 128], P('ctx')
The draws below stay inside these ranges and needn't reach their ends.
Inputs may be any that keep to these rules, and one draw needn't show every extreme that they name: Some key-value head has a window of 4 blocks.
All inputs are finite; a program needn't handle non-finite values.
Results may differ from the reference program's by a relative error of at most 0.019.
Values may be sent and summed in bfloat16 or wider, within the bound.
No kernel may reach another device: no remote copies, remote signals or barrier semaphores. Data moves between devices by JAX's collectives and lax.ppermute only.
A program may use at most 256 MiB of HBM per device.

```python
import math
import jax
import jax.numpy as jnp
from jax import lax

D = 128
HQ = 64
KVH = 8
TOK_DEV = 384
HOPS = 3
NBLK = 32
TOKENS = 12288


def drawn_keys(key):
    sample = jnp.clip(jax.random.normal(jax.random.fold_in(key, 11), (TOKENS, KVH, D), jnp.float32), -6.0, 6.0)
    return sample


def draw_key_heads(key, part):
    return drawn_keys(key).astype(jnp.bfloat16)


def draw_queries(key, part):
    sample = jnp.clip(jax.random.normal(jax.random.fold_in(key, 12), (TOKENS, HQ, D), jnp.float32), -6.0, 6.0)
    return sample.astype(jnp.bfloat16)


def draw_transforms(key, part):
    sample = jax.random.normal(jax.random.fold_in(key, 21), (NBLK, D, D), jnp.float32)
    orthogonal, triangle = jnp.linalg.qr(sample)
    gain_rows = jax.random.uniform(jax.random.fold_in(key, 22), (NBLK, 1, 1), jnp.float32, 0.85, 1.15)
    return orthogonal * gain_rows


def draw_window(key, part):
    sample = jax.random.randint(jax.random.fold_in(key, 31), (KVH,), 1, HOPS + 2)
    widest = jax.random.randint(jax.random.fold_in(key, 32), (), 0, KVH)
    return jnp.where(jnp.arange(KVH) == widest, HOPS + 1, sample).astype(jnp.int32)


def shard_levels(key, extent, cuts, low, top_value):
    gain, own = 1.0, jax.random.fold_in(key, 6)
    for dim, shards_of in cuts:
        heights = jnp.exp(jax.random.uniform(jax.random.fold_in(own, dim), (shards_of,), jnp.float32, low / len(cuts), top_value / len(cuts)))
        gain = gain * jnp.repeat(heights, extent[dim] // shards_of).reshape([-1 if axis == dim else 1 for axis in range(len(extent))])
    return gain


def scatter_about(stream_key, shape, deviation, bound, shards=(), kind=jnp.bfloat16):
    gain = shard_levels(stream_key, shape, shards, -0.22, 0.18) if shards else 1.0
    result = jax.random.normal(stream_key, shape, jnp.float32) * deviation * gain
    return jnp.minimum(jnp.maximum(result, -bound), bound).astype(kind)


def setup_inputs(seed: int = 0) -> dict:
    streams_of = jax.random.split(jax.random.key(seed), 8)
    queries = draw_queries(jax.random.fold_in(streams_of[7], 71), 0)
    key_heads = draw_key_heads(jax.random.fold_in(streams_of[7], 71), 0)
    value_heads = scatter_about(streams_of[2], (TOKENS, KVH, D), 1.0, 6.0, ((0, 32), (1, 4)))
    grad_out = scatter_about(streams_of[3], (TOKENS, HQ, D), 1.0, 6.0, ((0, 32), (1, 4)))
    transforms = draw_transforms(jax.random.fold_in(streams_of[7], 71), 0)
    window = draw_window(jax.random.fold_in(streams_of[7], 71), 0)
    first_block = jax.random.randint(streams_of[6], (1,), 0, NBLK).astype(jnp.int32)
    return {"queries": queries, "key_heads": key_heads, "value_heads": value_heads, "grad_out": grad_out, "transforms": transforms, "window": window, "first_block": first_block}


PRECISE = lax.Precision.HIGHEST

def halved(values_in):
    return lax.optimization_barrier(values_in.astype(jnp.bfloat16)).astype(jnp.float32)

def rotate_chain(keys_f, transforms):
    stacked = [keys_f]
    current = keys_f
    for hop_index in range(HOPS):
        turned = jnp.einsum('blgd,bed->blge', current, transforms, precision=PRECISE)
        current = jnp.roll(turned, 1, axis=0)
        stacked.append(current)
    return jnp.stack(stacked)

def reference(queries, key_heads, value_heads, grad_out, transforms, window, first_block):
    groups = HQ // KVH
    factor = 1.0 / math.sqrt(D)
    keys_f = key_heads.astype(jnp.float32).reshape(NBLK, TOK_DEV, KVH, D)
    visits = rotate_chain(keys_f, transforms)
    value_blocks = value_heads.reshape(NBLK, TOK_DEV, KVH, D)
    value_stack = jnp.stack([jnp.roll(value_blocks, hop_index, axis=0) for hop_index in range(HOPS + 1)])
    query_blocks = queries.reshape(NBLK, TOK_DEV, KVH, groups, D)
    grad_blocks = grad_out.reshape(NBLK, TOK_DEV, KVH, groups, D)
    position = (jnp.arange(NBLK).astype(jnp.int32) - first_block[0]) % NBLK
    hop_ids = jnp.arange(HOPS + 1).astype(jnp.int32)
    causal = jnp.arange(TOK_DEV)[:, None] >= jnp.arange(TOK_DEV)[None, :]
    causal_hops = (hop_ids[:, None, None] > 0) | causal[None]

    def one_block(block_index):
        query_f = query_blocks[block_index].astype(jnp.float32)
        grad_f = grad_blocks[block_index].astype(jnp.float32)
        key_tiles = halved(visits[:, block_index])
        value_f = value_stack[:, block_index].astype(jnp.float32)
        logits = jnp.einsum('lgjd,hmgd->hgjlm', query_f, key_tiles, precision=PRECISE) * factor
        usable = (hop_ids[:, None] < window[None, :]) & (position[block_index] - hop_ids >= 0)[:, None]
        keep_mask = usable[:, :, None, None, None] & causal_hops[:, None, None, :, :]
        logits = jnp.where(keep_mask, logits, -jnp.inf)
        row_max = lax.optimization_barrier(jnp.max(logits, axis=(0, 4)))
        row_total = lax.optimization_barrier(jnp.sum(jnp.exp(logits - row_max[None, :, :, :, None]), axis=(0, 4)))
        log_total = row_max + jnp.log(row_total)
        weights = jnp.exp(logits - log_total[None, :, :, :, None])
        slopes = jnp.einsum('lgjd,hmgd->hgjlm', grad_f, value_f, precision=PRECISE)
        row_dot = lax.optimization_barrier(jnp.sum(weights * slopes, axis=(0, 4)))
        score_half = halved(weights * (slopes - row_dot[None, :, :, :, None]))
        weight_half = halved(weights)
        query_grad = (jnp.einsum('hgjlm,hmgd->lgjd', score_half, key_tiles, precision=PRECISE) * factor).astype(jnp.bfloat16)
        tile_grad = jnp.einsum('hgjlm,lgjd->hmgd', score_half, query_f, precision=PRECISE) * factor
        value_part = jnp.einsum('hgjlm,lgjd->hmgd', weight_half, grad_f, precision=PRECISE)
        return (query_grad, tile_grad, value_part)
    query_grad, tile_grad, value_part = lax.map(one_block, jnp.arange(NBLK))
    rotated, pull = jax.vjp(rotate_chain, keys_f, transforms)
    key_grad, turn_grad = pull(jnp.swapaxes(tile_grad, 0, 1))
    value_grad = value_part[:, 0]
    for hop_index in range(1, HOPS + 1):
        value_grad = value_grad + jnp.roll(value_part[:, hop_index], -hop_index, axis=0)
    return (query_grad.reshape(TOKENS, HQ, D), key_grad.reshape(TOKENS, KVH, D).astype(jnp.bfloat16), value_grad.reshape(TOKENS, KVH, D).astype(jnp.bfloat16), turn_grad)
```

```python
import functools
import math

import jax
import jax.numpy as jnp
from jax import lax
from jax.experimental import pallas as pl
from jax.experimental.pallas import tpu as pltpu
from jax.sharding import PartitionSpec as P

HOPS = 3
F32 = jnp.float32
BF16 = jnp.bfloat16
LOG2E = math.log2(math.e)


def dot(a, b, ca, cb):
    return lax.dot_general(a, b, (((ca,), (cb,)), ((), ())), preferred_element_type=F32)


def dot_precise(a, b, ca, cb):
    return lax.dot_general(
        a, b, (((ca,), (cb,)), ((), ())), preferred_element_type=F32, precision=lax.Precision.HIGHEST
    )


def halves(x):
    upper = x.astype(BF16)
    return upper, (x - upper.astype(F32)).astype(BF16)


def shift(x, by):
    n = lax.axis_size("ctx")
    return lax.ppermute(x, "ctx", [(i, (i + by) % n) for i in range(n)])


def prepare(k_ref, v_ref, t_ref, a_ref, b_ref, wide, *, n):
    d = k_ref.shape[-1]
    for part, src in enumerate((k_ref, v_ref)):
        wide[...] = src[...].astype(F32)
        a_ref[part * n : (part + 1) * n] = wide[pl.ds(0, n, stride=2)].astype(BF16)
        b_ref[part * n : (part + 1) * n] = wide[pl.ds(1, n, stride=2)].astype(BF16)
    upper, lower = halves(t_ref[...])
    a_ref[2 * n : 2 * n + d] = upper
    a_ref[2 * n + d : 2 * n + 2 * d] = lower


def attend(
    scal, q_ref, do_ref, own_ref, r1_ref, r2_ref, r3_ref, t1_ref, t2_ref, t3_ref, prev_dm, prev_dq,
    dq_ref, y0_ref, y1_ref, y2_ref, y3_ref, dm_ref,
    prod, keys, keys_t, dk, dv, e_ref, p_ref, stat, dq_acc,
    *, head, rows, n, d, hops, steps,
):
    step = pl.program_id(0)
    R = rows * q_ref.shape[1]
    group = q_ref.shape[1]
    factor = 1.0 / math.sqrt(d)
    c2 = factor * LOG2E
    live = jnp.minimum(scal[head], scal[2] + 1)
    sources = (own_ref, r1_ref, r2_ref, r3_ref)

    @pl.when(step == 0)
    def _():
        dk[...] = jnp.zeros_like(dk)
        dv[...] = jnp.zeros_like(dv)
        total = None
        for h in range(hops + 1):
            raw = sources[h][0:n]
            if h == 0:
                tile = raw
            else:
                t_ref = (t1_ref, t2_ref, t3_ref)[h - 1]
                mat = t_ref[0:d].astype(F32) + t_ref[d : 2 * d].astype(F32)
                total = mat if total is None else dot_precise(total, mat, 1, 0)
                prod[h - 1] = total
                upper, lower = halves(total)
                tile = (dot(raw, upper, 1, 1) + dot(raw, lower, 1, 1)).astype(BF16)
            keys[h] = tile
            keys_t[h] = tile.T

    q = q_ref[...].reshape(R, d)
    do = do_ref[...].reshape(R, d)

    def forward(h, m, l, r):
        s = dot(keys[h], q, 1, 1)
        dp = dot(sources[h][n : 2 * n], do, 1, 1)
        if h == 0:
            key = lax.broadcasted_iota(jnp.int32, (n, R), 0)
            row = step * rows + lax.broadcasted_iota(jnp.int32, (n, R), 1) // group
            s = jnp.where(key <= row, s, -jnp.inf)
        m2 = jnp.max(s, axis=0, keepdims=True)
        if h:
            m2 = jnp.maximum(m, m2)
        e = jnp.exp2((s - m2) * c2)
        ls = jnp.sum(e, axis=0, keepdims=True)
        rs = jnp.sum(e * dp, axis=0, keepdims=True)
        if h:
            a = jnp.exp2((m - m2) * c2)
            ls = l * a + ls
            rs = r * a + rs
        e_ref[h] = e
        p_ref[h] = dp
        stat[h] = m2
        stat[4] = m2
        stat[5] = ls
        stat[6] = rs

    forward(0, None, None, None)
    for h in range(1, hops + 1):

        @pl.when(h < live)
        def _(h=h):
            forward(h, stat[4], stat[5], stat[6])

    m = stat[4]
    inv = 1.0 / stat[5]
    r = stat[6] * inv

    def backward(h):
        w = e_ref[h] * (jnp.exp2((stat[h] - m) * c2) * inv)
        ds = (w * (p_ref[h] - r)).astype(BF16)
        dv[h] += dot(w.astype(BF16), do, 1, 0)
        dk[h] += dot(ds, q, 1, 0)
        return dot(keys_t[h], ds, 1, 0)

    dq_acc[...] = backward(0)
    for h in range(1, hops + 1):

        @pl.when(h < live)
        def _(h=h):
            dq_acc[...] += backward(h)

    dq_ref[...] = (dq_acc[...] * factor).T.astype(BF16).reshape(rows, group, d)

    @pl.when(step == steps - 1)
    def _():
        y0_ref[0:n] = dk[0] * factor
        y0_ref[n : 2 * n] = dv[0]
        for h, y_ref in ((1, y1_ref), (2, y2_ref), (3, y3_ref)):
            g_up, g_lo = halves(dk[h] * factor)
            p_up, p_lo = halves(prod[h - 1])
            back = dot(g_up, p_up, 1, 0) + dot(g_up, p_lo, 1, 0) + dot(g_lo, p_up, 1, 0)
            y_ref[0:n] = back.astype(BF16)
            y_ref[n : 2 * n] = dv[h].astype(BF16)
            raw = sources[h][0:n]
            dm_ref[h - 1] = dot(g_up, raw, 0, 0) + dot(g_lo, raw, 0, 0)
        if prev_dm is not None:
            t1, t2, t3 = [
                t[0:d].astype(F32) + t[d : 2 * d].astype(F32) for t in (t1_ref, t2_ref, t3_ref)
            ]
            dm1, dm2, dm3 = [dm_ref[i] + prev_dm[i] for i in range(3)]
            mid = dm2 + dot_precise(dm3, t3, 1, 1)
            dm_ref[0] = dm1 + dot_precise(mid, t2, 1, 1)
            dm_ref[1] = dot_precise(t1, mid, 0, 0)
            dm_ref[2] = dot_precise(prod[1], dm3, 0, 0)


def attend_first(scal, q, do, own, r1, r2, r3, *rest, **kw):
    attend(scal, q, do, own, r1, r2, r3, r1.at[768:1024], r2.at[768:1024], r3.at[768:1024], None, None, *rest, **kw)


def finish(*refs, n):
    own_a, own_b = refs[0:2]
    back = (refs[2:5], refs[5:8])
    outs = refs[8:10]
    wide = refs[10]
    for part in range(2):
        lo, hi = part * n, (part + 1) * n
        for g, own in enumerate((own_a, own_b)):
            total = own[lo:hi]
            for b in back[g]:
                total = total + b[lo:hi].astype(F32)
            wide[pl.ds(g, n, stride=2)] = total
        outs[part][...] = wide[...].astype(BF16)


def whole(shape):
    return pl.BlockSpec(shape, lambda *a: (0,) * len(shape))


def shards(queries, key_heads, value_heads, grad_out, transforms, window, first_block):
    n, heads, d = queries.shape
    kv = key_heads.shape[1]
    group = heads // kv
    blocks = lax.axis_size("ctx")
    position = (lax.axis_index("ctx") - first_block[0]) % blocks
    scal = jnp.concatenate([window, position[None]]).astype(jnp.int32)
    q4 = queries.reshape(n, kv, group, d)
    do4 = grad_out.reshape(n, kv, group, d)
    vmem = pltpu.CompilerParams(vmem_limit_bytes=60 << 20)

    buf_a, buf_b = pl.pallas_call(
        functools.partial(prepare, n=n),
        out_shape=[jax.ShapeDtypeStruct((2 * n + 2 * d, d), BF16), jax.ShapeDtypeStruct((2 * n, d), BF16)],
        scratch_shapes=[pltpu.VMEM((2 * n, d), F32)],
        name="prepare",
    )(key_heads.reshape(2 * n, d), value_heads.reshape(2 * n, d), transforms[0])

    arr_a = [shift(buf_a, h) for h in range(1, HOPS + 1)]
    buf_b, *arr_a = lax.optimization_barrier((buf_b, *arr_a))
    arr_b = [shift(buf_b, h) for h in range(1, HOPS + 1)]

    rows = n // 2
    steps = n // rows
    R = rows * group

    def call(head, own, arrived, extra):
        first = head == 0
        blk = pl.BlockSpec((rows, None, group, d), lambda c, s: (c, head, 0, 0))
        in_specs = [blk, blk, whole(own.shape)] + [whole(a.shape) for a in arrived]
        args = [q4, do4, own, *arrived]
        alias = {}
        if not first:
            prev_dq, prev_dm, turns = extra
            turn_spec = pl.BlockSpec((2 * d, d), lambda c, s: (n // d, 0))
            in_specs += [turn_spec] * HOPS + [whole(prev_dm.shape), pl.BlockSpec(memory_space=pl.ANY)]
            args += [*turns, prev_dm, prev_dq]
            alias = {len(args): 0}
        yshape = jax.ShapeDtypeStruct((2 * n, d), BF16)
        return pl.pallas_call(
            functools.partial(
                attend_first if first else attend, head=head, rows=rows, n=n, d=d, hops=HOPS, steps=steps
            ),
            grid_spec=pltpu.PrefetchScalarGridSpec(
                num_scalar_prefetch=1,
                grid=(steps,),
                in_specs=in_specs,
                out_specs=[blk, whole((2 * n, d))] + [whole((2 * n, d))] * HOPS + [whole((HOPS, d, d))],
                scratch_shapes=[
                    pltpu.VMEM((HOPS, d, d), F32),
                    pltpu.VMEM((HOPS + 1, n, d), BF16),
                    pltpu.VMEM((HOPS + 1, d, n), BF16),
                    pltpu.VMEM((HOPS + 1, n, d), F32),
                    pltpu.VMEM((HOPS + 1, n, d), F32),
                    pltpu.VMEM((HOPS + 1, n, R), F32),
                    pltpu.VMEM((HOPS + 1, n, R), F32),
                    pltpu.VMEM((8, 1, R), F32),
                    pltpu.VMEM((d, R), F32),
                ],
            ),
            out_shape=[
                jax.ShapeDtypeStruct((n, kv, group, d), BF16),
                jax.ShapeDtypeStruct((2 * n, d), F32),
                yshape, yshape, yshape,
                jax.ShapeDtypeStruct((HOPS, d, d), F32),
            ],
            input_output_aliases=alias,
            compiler_params=vmem,
            cost_estimate=pl.CostEstimate(flops=12_000_000_000, bytes_accessed=6_000_000, transcendentals=5_000_000),
            name="attend%d" % head,
        )(scal, *args)

    dq, own_a, *ys_a, dm_a = call(0, buf_a, arr_a, None)
    back_a = [shift(y, -h - 1) for h, y in enumerate(ys_a)]
    dq, own_b, *ys_b, dm_b = call(1, buf_b, arr_b, (dq, dm_a, arr_a))
    dt = [shift(dm_b[i].astype(BF16), -i - 1) for i in range(HOPS)]
    back_b = [shift(y, -h - 1) for h, y in enumerate(ys_b)]
    turn = dt[0].astype(F32) + dt[1].astype(F32) + dt[2].astype(F32)
    peers = lax.axis_size("kv")
    total = turn
    for k in range(1, peers):
        sent = lax.ppermute(turn.astype(BF16), "kv", [(i, (i + k) % peers) for i in range(peers)])
        total = total + sent.astype(F32)

    key_grad, value_grad = pl.pallas_call(
        functools.partial(finish, n=n),
        out_shape=[jax.ShapeDtypeStruct((2 * n, d), BF16)] * 2,
        scratch_shapes=[pltpu.VMEM((2 * n, d), F32)],
        name="finish",
    )(own_a, own_b, *back_a, *back_b)
    return (
        dq.reshape(n, heads, d),
        key_grad.reshape(n, kv, d),
        value_grad.reshape(n, kv, d),
        total[None],
    )


def solution(mesh):
    return jax.shard_map(
        shards,
        mesh=mesh,
        in_specs=(
            P("ctx", "kv", None),
            P("ctx", "kv", None),
            P("ctx", "kv", None),
            P("ctx", "kv", None),
            P("ctx", None, None),
            P("kv"),
            P(),
        ),
        out_specs=(
            P("ctx", "kv", None),
            P("ctx", "kv", None),
            P("ctx", "kv", None),
            P("ctx", None, None),
        ),
        check_vma=False,
    )
```

```python
import functools
import math

import jax
import jax.numpy as jnp
from jax import lax
from jax.experimental import pallas as pl
from jax.experimental.pallas import tpu as pltpu
from jax.sharding import PartitionSpec as P

HOPS = 3
F32 = jnp.float32
BF16 = jnp.bfloat16
LOG2E = math.log2(math.e)


def dot(a, b, ca, cb):
    return lax.dot_general(a, b, (((ca,), (cb,)), ((), ())), preferred_element_type=F32)


def dot_precise(a, b, ca, cb):
    return lax.dot_general(
        a, b, (((ca,), (cb,)), ((), ())), preferred_element_type=F32, precision=lax.Precision.HIGHEST
    )


def halves(x):
    upper = x.astype(BF16)
    return upper, (x - upper.astype(F32)).astype(BF16)


def shift(x, by):
    n = lax.axis_size("ctx")
    return lax.ppermute(x, "ctx", [(i, (i + by) % n) for i in range(n)])


def prepare(k_ref, v_ref, t_ref, a_ref, b_ref, own_ref, wide, *, n):
    d = k_ref.shape[-1]
    for part, src in enumerate((k_ref, v_ref)):
        wide[...] = src[...].astype(F32)
        for g, out in enumerate((a_ref, b_ref)):
            rows = wide[pl.ds(g, n, stride=2)].astype(BF16)
            out[part * n : (part + 1) * n] = rows
            own_ref[g, part * n : (part + 1) * n] = rows
    upper, lower = halves(t_ref[...])
    a_ref[2 * n : 2 * n + d] = upper
    a_ref[2 * n + d : 2 * n + 2 * d] = lower


def diagonal(s, first, group):
    key = lax.broadcasted_iota(jnp.int32, s.shape, 0)
    row = first + lax.broadcasted_iota(jnp.int32, s.shape, 1) // group
    return jnp.where(key <= row, s, -jnp.inf)


def near_stats(q_ref, do_ref, own_ref, stat_ref, *, n, d, cut, c2):
    group = q_ref.shape[1]
    for c in range(n // cut):
        lo, hi = c * cut, (c + 1) * cut
        q = q_ref[lo:hi].reshape(cut * group, d)
        do = do_ref[lo:hi].reshape(cut * group, d)
        s = diagonal(dot(own_ref[0:hi], q, 1, 1), lo, group)
        dp = dot(own_ref[n : n + hi], do, 1, 1)
        m = jnp.max(s, axis=0, keepdims=True)
        e = jnp.exp2((s - m) * c2)
        cols = slice(lo * group, hi * group)
        stat_ref[0:1, cols] = m
        stat_ref[1:2, cols] = jnp.sum(e, axis=0, keepdims=True)
        stat_ref[2:3, cols] = jnp.sum(e * dp, axis=0, keepdims=True)


def far(
    win, fst, q_ref, do_ref, r1_ref, r2_ref, r3_ref, t1_ref, t2_ref, t3_ref, near_ref, *rest,
    head, n, d, hops, c2, factor, blocks,
):
    if head:
        prev_dm, rest = rest[0], rest[3:]
    dq_ref, stat_ref, y1_ref, y2_ref, y3_ref = rest[0:5]
    dm_refs = rest[5:-9]
    prod, keys, vals, keys_t, dk, dv, e_ref, p_ref, tops = rest[-9:]
    group = q_ref.shape[1]
    R = n * group
    place = lax.rem(lax.axis_index("ctx") - fst[0] + blocks, blocks)
    live = jnp.minimum(win[head], place + 1) - 1
    sources = (r1_ref, r2_ref, r3_ref)
    turns = (t1_ref, t2_ref, t3_ref)

    dk[...] = jnp.zeros_like(dk)
    dv[...] = jnp.zeros_like(dv)
    total = None
    for i in range(hops):
        mat = turns[i][0:d].astype(F32) + turns[i][d : 2 * d].astype(F32)
        total = mat if total is None else dot_precise(total, mat, 1, 0)
        prod[i] = total
        upper, lower = halves(total)
        raw = sources[i][0:n]
        tile = (dot(raw, upper, 1, 1) + dot(raw, lower, 1, 1)).astype(BF16)
        keys[i] = tile
        keys_t[i] = tile.T
        vals[i] = sources[i][n : 2 * n]
    stat_ref[...] = near_ref[...]
    dq_ref[...] = jnp.zeros_like(dq_ref)

    def forward(i, carry):
        q = q_ref[...].reshape(R, d)
        do = do_ref[...].reshape(R, d)
        s = dot(keys[i], q, 1, 1)
        dp = dot(vals[i], do, 1, 1)
        m = stat_ref[0:1]
        m2 = jnp.maximum(m, jnp.max(s, axis=0, keepdims=True))
        e = jnp.exp2((s - m2) * c2)
        a = jnp.exp2((m - m2) * c2)
        stat_ref[1:2] = stat_ref[1:2] * a + jnp.sum(e, axis=0, keepdims=True)
        stat_ref[2:3] = stat_ref[2:3] * a + jnp.sum(e * dp, axis=0, keepdims=True)
        stat_ref[0:1] = m2
        tops[i] = m2
        e_ref[i] = e
        p_ref[i] = dp
        return carry

    lax.fori_loop(0, live, forward, 0)
    inv = 1.0 / stat_ref[1:2]
    stat_ref[1:2] = inv
    stat_ref[2:3] = stat_ref[2:3] * inv

    def backward(i, carry):
        q = q_ref[...].reshape(R, d)
        do = do_ref[...].reshape(R, d)
        w = e_ref[i] * (jnp.exp2((tops[i] - stat_ref[0:1]) * c2) * stat_ref[1:2])
        ds = (w * (p_ref[i] - stat_ref[2:3])).astype(BF16)
        dv[i] = dot(w.astype(BF16), do, 1, 0)
        dk[i] = dot(ds, q, 1, 0)
        dq_ref[...] += dot(keys_t[i], ds, 1, 0)
        return carry

    lax.fori_loop(0, live, backward, 0)

    grads = []
    for i, y_ref in enumerate((y1_ref, y2_ref, y3_ref)):
        g_up, g_lo = halves(dk[i] * factor)
        p_up, p_lo = halves(prod[i])
        back = dot(g_up, p_up, 1, 0) + dot(g_up, p_lo, 1, 0) + dot(g_lo, p_up, 1, 0)
        y_ref[0:n] = back.astype(BF16)
        y_ref[n : 2 * n] = dv[i].astype(BF16)
        raw = sources[i][0:n]
        grads.append(dot(g_up, raw, 0, 0) + dot(g_lo, raw, 0, 0))
    if head:
        t2, t3 = [t[0:d].astype(F32) + t[d : 2 * d].astype(F32) for t in turns[1:]]
        dm1, dm2, dm3 = [grads[i] + prev_dm[i] for i in range(3)]
        mid = dm2 + dot_precise(dm3, t3, 1, 1)
        dm_refs[0][...] = (dm1 + dot_precise(mid, t2, 1, 1)).astype(BF16)
        dm_refs[1][...] = dot_precise(prod[0], mid, 0, 0).astype(BF16)
        dm_refs[2][...] = dot_precise(prod[1], dm3, 0, 0).astype(BF16)
    else:
        for i in range(hops):
            dm_refs[0][i] = grads[i]


def near(q_ref, do_ref, own_ref, stat_ref, far_ref, dq_ref, y_ref, *, n, d, cut, c2, factor):
    group = q_ref.shape[1]
    keys_t = own_ref[0:n].T
    for c in reversed(range(n // cut)):
        lo, hi = c * cut, (c + 1) * cut
        cols = slice(lo * group, hi * group)
        q = q_ref[lo:hi].reshape(cut * group, d)
        do = do_ref[lo:hi].reshape(cut * group, d)
        s = diagonal(dot(own_ref[0:hi], q, 1, 1), lo, group)
        dp = dot(own_ref[n : n + hi], do, 1, 1)
        w = jnp.exp2((s - stat_ref[0:1, cols]) * c2) * stat_ref[1:2, cols]
        ds = (w * (dp - stat_ref[2:3, cols])).astype(BF16)
        dv = dot(w.astype(BF16), do, 1, 0)
        dk = dot(ds, q, 1, 0)
        if hi == n:
            y_ref[0:n] = dk
            y_ref[n : 2 * n] = dv
        else:
            y_ref[0:hi] += dk
            y_ref[n : n + hi] += dv
        dq = far_ref[:, cols] + dot(keys_t[:, 0:hi], ds, 1, 0)
        dq_ref[lo:hi] = (dq * factor).T.astype(BF16).reshape(cut, group, d)
    y_ref[0:n] = y_ref[0:n] * factor


def finish(own_ref, *refs, n):
    back = (refs[0:3], refs[3:6])
    outs = refs[6:8]
    wide = refs[8]
    for part in range(2):
        lo, hi = part * n, (part + 1) * n
        for g in range(2):
            total = own_ref[g, lo:hi]
            for b in back[g]:
                total = total + b[lo:hi].astype(F32)
            wide[pl.ds(g, n, stride=2)] = total
        outs[part][...] = wide[...].astype(BF16)


def whole(shape):
    return pl.BlockSpec(shape, lambda *a: (0,) * len(shape))


def cost(flops, size):
    return pl.CostEstimate(flops=flops, bytes_accessed=size, transcendentals=0)


def shards(queries, key_heads, value_heads, grad_out, transforms, window, first_block):
    n, heads, d = queries.shape
    kv = key_heads.shape[1]
    group = heads // kv
    R = n * group
    blocks = lax.axis_size("ctx")
    factor = 1.0 / math.sqrt(d)
    c2 = factor * LOG2E
    cut = n // 4
    q4 = queries.reshape(n, kv, group, d)
    do4 = grad_out.reshape(n, kv, group, d)

    buf_a, buf_b, own = pl.pallas_call(
        functools.partial(prepare, n=n),
        out_shape=[
            jax.ShapeDtypeStruct((2 * n + 2 * d, d), BF16),
            jax.ShapeDtypeStruct((2 * n, d), BF16),
            jax.ShapeDtypeStruct((kv, 2 * n, d), BF16),
        ],
        scratch_shapes=[pltpu.VMEM((2 * n, d), F32)],
        name="prepare",
    )(key_heads.reshape(2 * n, d), value_heads.reshape(2 * n, d), transforms[0])

    arr_a = []
    for h in range(1, HOPS + 1):
        arr_a.append(shift(buf_a, h))

    rows_blk = pl.BlockSpec((n, None, group, d), lambda g: (0, g, 0, 0))
    own_blk = pl.BlockSpec((None, 2 * n, d), lambda g: (g, 0, 0))
    stat_blk = pl.BlockSpec((None, 8, R), lambda g: (g, 0, 0))
    stats0 = pl.pallas_call(
        functools.partial(near_stats, n=n, d=d, cut=cut, c2=c2),
        grid=(kv,),
        in_specs=[rows_blk, rows_blk, own_blk],
        out_specs=stat_blk,
        out_shape=jax.ShapeDtypeStruct((kv, 8, R), F32),
        cost_estimate=cost(2_500_000_000, 6_000_000),
        name="near_stats",
    )(q4, do4, own)

    buf_b, *arr_a = lax.optimization_barrier((buf_b, *arr_a))
    arr_b = []
    for h in range(1, HOPS + 1):
        arr_b.append(shift(buf_b, h))

    def call(head, arrived, extra):
        blk = pl.BlockSpec((n, None, group, d), lambda c, *s: (0, head, 0, 0))
        st = pl.BlockSpec((None, 8, R), lambda c, *s: (head, 0, 0))
        turn_spec = pl.BlockSpec((2 * d, d), lambda c, *s: (n // d, 0))
        row_spec = pl.BlockSpec((2 * n, d), lambda c, *s: (0, 0))
        in_specs = [blk, blk] + [row_spec] * HOPS + [turn_spec] * HOPS + [st]
        args = [q4, do4, *arrived, *arr_a, stats0]
        alias = {}
        dms = [jax.ShapeDtypeStruct((d, d), BF16)] * HOPS
        if head:
            prev_dq, prev_st, prev_dm = extra
            in_specs += [whole(prev_dm.shape)] + [pl.BlockSpec(memory_space=pl.ANY)] * 2
            args += [prev_dm, prev_dq, prev_st]
            alias = {len(args): 0, len(args) + 1: 1}
        else:
            dms = [jax.ShapeDtypeStruct((HOPS, d, d), F32)]
        yshape = jax.ShapeDtypeStruct((2 * n, d), BF16)
        return pl.pallas_call(
            functools.partial(
                far,
                head=head, n=n, d=d, hops=HOPS, c2=c2, factor=factor, blocks=blocks,
            ),
            grid_spec=pltpu.PrefetchScalarGridSpec(
                num_scalar_prefetch=2,
                grid=(1,),
                in_specs=in_specs,
                out_specs=[pl.BlockSpec((None, d, R), lambda c, *s: (head, 0, 0)), st]
                + [whole((2 * n, d))] * HOPS
                + [whole(x.shape) for x in dms],
                scratch_shapes=[
                    pltpu.VMEM((HOPS, d, d), F32),
                    pltpu.VMEM((HOPS, n, d), BF16),
                    pltpu.VMEM((HOPS, n, d), BF16),
                    pltpu.VMEM((HOPS, d, n), BF16),
                    pltpu.VMEM((HOPS, n, d), F32),
                    pltpu.VMEM((HOPS, n, d), F32),
                    pltpu.VMEM((HOPS, n, R), F32),
                    pltpu.VMEM((HOPS, n, R), F32),
                    pltpu.VMEM((HOPS, 1, R), F32),
                ],
            ),
            out_shape=[
                jax.ShapeDtypeStruct((kv, d, R), F32),
                jax.ShapeDtypeStruct((kv, 8, R), F32),
                yshape, yshape, yshape, *dms,
            ],
            input_output_aliases=alias,
            compiler_params=pltpu.CompilerParams(vmem_limit_bytes=56 << 20),
            cost_estimate=cost(9_000_000_000, 6_000_000),
        )(window, first_block, *args)

    dq, st, *ys_a, dm_a = call(0, arr_a, None)
    back_a = []
    for h in range(HOPS):
        back_a.append(shift(ys_a[h], -h - 1))
    dq, st, y1, y2, y3, *dms = call(1, arr_b, (dq, st, dm_a))
    dt, back_b = [], []
    for h in range(HOPS):
        dt.append(shift(dms[h], -h - 1))
    for h, y in enumerate((y1, y2, y3)):
        back_b.append(shift(y, -h - 1))

    dq_out, own_grad = pl.pallas_call(
        functools.partial(near, n=n, d=d, cut=cut, c2=c2, factor=factor),
        grid=(kv,),
        in_specs=[rows_blk, rows_blk, own_blk, stat_blk, pl.BlockSpec((None, d, R), lambda g: (g, 0, 0))],
        out_specs=[rows_blk, own_blk],
        out_shape=[
            jax.ShapeDtypeStruct((n, kv, group, d), BF16),
            jax.ShapeDtypeStruct((kv, 2 * n, d), F32),
        ],
        cost_estimate=cost(5_000_000_000, 9_000_000),
        name="near",
    )(q4, do4, own, st, dq)

    turn = dt[0].astype(F32) + dt[1].astype(F32) + dt[2].astype(F32)
    peers = lax.axis_size("kv")
    half = turn.astype(BF16)
    total = turn
    for k in range(1, peers):
        sent = lax.ppermute(half, "kv", [(i, (i + k) % peers) for i in range(peers)])
        total = total + sent.astype(F32)

    key_grad, value_grad = pl.pallas_call(
        functools.partial(finish, n=n),
        out_shape=[jax.ShapeDtypeStruct((2 * n, d), BF16)] * 2,
        scratch_shapes=[pltpu.VMEM((2 * n, d), F32)],
        name="finish",
    )(own_grad, *back_a, *back_b)
    return (
        dq_out.reshape(n, heads, d),
        key_grad.reshape(n, kv, d),
        value_grad.reshape(n, kv, d),
        total[None],
    )


def solution(mesh):
    return jax.shard_map(
        shards,
        mesh=mesh,
        in_specs=(
            P("ctx", "kv", None),
            P("ctx", "kv", None),
            P("ctx", "kv", None),
            P("ctx", "kv", None),
            P("ctx", None, None),
            P("kv"),
            P(),
        ),
        out_specs=(
            P("ctx", "kv", None),
            P("ctx", "kv", None),
            P("ctx", "kv", None),
            P("ctx", None, None),
        ),
        check_vma=False,
    )
```

```python
import functools
import math

import jax
import jax.numpy as jnp
from jax import lax
from jax.experimental import pallas as pl
from jax.experimental.pallas import tpu as pltpu
from jax.sharding import PartitionSpec as P

HOPS = 3
F32 = jnp.float32
BF16 = jnp.bfloat16
LOG2E = math.log2(math.e)


def dot(a, b, ca, cb):
    return lax.dot_general(a, b, (((ca,), (cb,)), ((), ())), preferred_element_type=F32)


def halves(x):
    upper = x.astype(BF16)
    return upper, (x - upper.astype(F32)).astype(BF16)


def dot_split(a, b, ca, cb):
    upper, lower = halves(a)
    return dot(upper, b, ca, cb) + dot(lower, b, ca, cb)


def shift(x, by):
    n = lax.axis_size("ctx")
    return lax.ppermute(x, "ctx", [(i, (i + by) % n) for i in range(n)])


def prepare(k_ref, v_ref, t_ref, a_ref, b_ref, own_ref, wide, *, n):
    d = k_ref.shape[-1]
    for part, src in enumerate((k_ref, v_ref)):
        wide[...] = src[...].astype(F32)
        for g, out in enumerate((a_ref, b_ref)):
            rows = wide[pl.ds(g, n, stride=2)].astype(BF16)
            out[part * n : (part + 1) * n] = rows
            own_ref[g, part * n : (part + 1) * n] = rows
    a_ref[2 * n : 2 * n + d] = t_ref[...].astype(BF16)


def diagonal(s, first, group):
    key = lax.broadcasted_iota(jnp.int32, s.shape, 0)
    row = first + lax.broadcasted_iota(jnp.int32, s.shape, 1) // group
    return jnp.where(key <= row, s, -jnp.inf)


def near_stats(q_ref, do_ref, own_ref, stat_ref, *, n, d, cut, c2):
    group = q_ref.shape[1]
    for c in range(n // cut):
        lo, hi = c * cut, (c + 1) * cut
        q = q_ref[lo:hi].reshape(cut * group, d)
        do = do_ref[lo:hi].reshape(cut * group, d)
        s = diagonal(dot(own_ref[0:hi], q, 1, 1), lo, group)
        dp = dot(own_ref[n : n + hi], do, 1, 1)
        m = jnp.max(s, axis=0, keepdims=True)
        e = jnp.exp2((s - m) * c2)
        cols = slice(lo * group, hi * group)
        stat_ref[0:1, cols] = m
        stat_ref[1:2, cols] = jnp.sum(e, axis=0, keepdims=True)
        stat_ref[2:3, cols] = jnp.sum(e * dp, axis=0, keepdims=True)


def far(
    win, fst, q_ref, do_ref, r1_ref, r2_ref, r3_ref, t1_ref, t2_ref, t3_ref, near_ref, *rest,
    head, n, d, hops, c2, factor, blocks,
):
    if head:
        prev_dm, rest = rest[0], rest[3:]
    dq_ref, stat_ref, y1_ref, y2_ref, y3_ref = rest[0:5]
    dm_refs = rest[5:-12]
    prod, keys, vals, keys_t, dk, dv, e_ref, p_ref, tops, q_buf, do_buf, sems = rest[-12:]
    group = q_ref.shape[2]
    R = n * group
    place = lax.rem(lax.axis_index("ctx") - fst[0] + blocks, blocks)
    live = jnp.minimum(win[head], place + 1) - 1
    sources = (r1_ref, r2_ref, r3_ref)
    turns = (t1_ref, t2_ref, t3_ref)

    copies = [
        pltpu.make_async_copy(src.at[:, head], dst, sems.at[k])
        for k, (src, dst) in enumerate(((q_ref, q_buf), (do_ref, do_buf)))
    ]
    for copy in copies:
        copy.start()
    dk[...] = jnp.zeros_like(dk)
    dv[...] = jnp.zeros_like(dv)
    total = None
    for i in range(hops):
        mat = turns[i][...]
        total = mat.astype(F32) if total is None else dot_split(total, mat, 1, 0)
        upper, lower = halves(total)
        prod[i] = upper
        raw = sources[i][0:n]
        tile = dot(raw, upper, 1, 1)
        if i:
            tile = tile + dot(raw, lower, 1, 1)
        tile = tile.astype(BF16)
        keys[i] = tile
        keys_t[i] = tile.T
        vals[i] = sources[i][n : 2 * n]
    stat_ref[...] = near_ref[...]
    dq_ref[...] = jnp.zeros_like(dq_ref)
    for copy in copies:
        copy.wait()

    def forward(i, carry):
        q = q_buf[...].reshape(R, d)
        do = do_buf[...].reshape(R, d)
        s = dot(keys[i], q, 1, 1)
        dp = dot(vals[i], do, 1, 1)
        m = stat_ref[0:1]
        m2 = jnp.maximum(m, jnp.max(s, axis=0, keepdims=True))
        e = jnp.exp2((s - m2) * c2)
        a = jnp.exp2((m - m2) * c2)
        stat_ref[1:2] = stat_ref[1:2] * a + jnp.sum(e, axis=0, keepdims=True)
        stat_ref[2:3] = stat_ref[2:3] * a + jnp.sum(e * dp, axis=0, keepdims=True)
        stat_ref[0:1] = m2
        tops[i] = m2
        e_ref[i] = e
        p_ref[i] = dp
        return carry

    lax.fori_loop(0, live, forward, 0)
    inv = 1.0 / stat_ref[1:2]
    stat_ref[1:2] = inv
    stat_ref[2:3] = stat_ref[2:3] * inv

    def backward(i, carry):
        q = q_buf[...].reshape(R, d)
        do = do_buf[...].reshape(R, d)
        w = e_ref[i] * (jnp.exp2((tops[i] - stat_ref[0:1]) * c2) * stat_ref[1:2])
        ds = (w * (p_ref[i] - stat_ref[2:3])).astype(BF16)
        dv[i] = dot(w.astype(BF16), do, 1, 0)
        dk[i] = dot(ds, q, 1, 0)
        dq_ref[...] += dot(keys_t[i], ds, 1, 0)
        return carry

    lax.fori_loop(0, live, backward, 0)

    grads = []
    for i, y_ref in enumerate((y1_ref, y2_ref, y3_ref)):
        g = (dk[i] * factor).astype(BF16)
        y_ref[0:n] = dot(g, prod[i], 1, 0).astype(BF16)
        y_ref[n : 2 * n] = dv[i].astype(BF16)
        grads.append(dot(g, sources[i][0:n], 0, 0))
    if head:
        dm1, dm2, dm3 = [grads[i] + prev_dm[i] for i in range(3)]
        mid = dm2 + dot_split(dm3, turns[2][...], 1, 1)
        y1_ref[2 * n : 2 * n + d] = (dm1 + dot_split(mid, turns[1][...], 1, 1)).astype(BF16)
        y2_ref[2 * n : 2 * n + d] = dot(turns[0][...], mid.astype(BF16), 0, 0).astype(BF16)
        y3_ref[2 * n : 2 * n + d] = dot(prod[1], dm3.astype(BF16), 0, 0).astype(BF16)
    else:
        for i in range(hops):
            dm_refs[0][i] = grads[i]


def near(q_ref, do_ref, own_ref, stat_ref, far_ref, dq_ref, y_ref, *, n, d, cut, c2, factor):
    group = q_ref.shape[1]
    keys_t = own_ref[0:n].T
    for c in reversed(range(n // cut)):
        lo, hi = c * cut, (c + 1) * cut
        cols = slice(lo * group, hi * group)
        q = q_ref[lo:hi].reshape(cut * group, d)
        do = do_ref[lo:hi].reshape(cut * group, d)
        s = diagonal(dot(own_ref[0:hi], q, 1, 1), lo, group)
        dp = dot(own_ref[n : n + hi], do, 1, 1)
        w = jnp.exp2((s - stat_ref[0:1, cols]) * c2) * stat_ref[1:2, cols]
        ds = (w * (dp - stat_ref[2:3, cols])).astype(BF16)
        dv = dot(w.astype(BF16), do, 1, 0)
        dk = dot(ds, q, 1, 0)
        if hi == n:
            y_ref[0:n] = dk
            y_ref[n : 2 * n] = dv
        else:
            y_ref[0:hi] += dk
            y_ref[n : n + hi] += dv
        dq = far_ref[:, cols] + dot(keys_t[:, 0:hi], ds, 1, 0)
        dq_ref[lo:hi] = (dq * factor).T.astype(BF16).reshape(cut, group, d)
    y_ref[0:n] = y_ref[0:n] * factor


def finish(own_ref, *refs, n):
    back, outs, wide = (refs[0:3], refs[3:6]), refs[6:8], refs[8]
    for part in range(2):
        rows = slice(part * n, (part + 1) * n)
        for g in range(2):
            total = own_ref[g, rows]
            for ref in back[g]:
                total = total + ref[rows].astype(F32)
            wide[pl.ds(g, n, stride=2)] = total
        outs[part][...] = wide[...].astype(BF16)


def whole(shape):
    return pl.BlockSpec(shape, lambda *a: (0,) * len(shape))


def cost(flops, size):
    return pl.CostEstimate(flops=flops, bytes_accessed=size, transcendentals=0)


def shards(queries, key_heads, value_heads, grad_out, transforms, window, first_block):
    n, heads, d = queries.shape
    kv = key_heads.shape[1]
    group = heads // kv
    R = n * group
    blocks = lax.axis_size("ctx")
    factor = 1.0 / math.sqrt(d)
    c2 = factor * LOG2E
    cut = n // 4
    q4 = queries.reshape(n, kv, group, d)
    do4 = grad_out.reshape(n, kv, group, d)

    buf_a, buf_b, own = pl.pallas_call(
        functools.partial(prepare, n=n),
        out_shape=[
            jax.ShapeDtypeStruct((2 * n + d, d), BF16),
            jax.ShapeDtypeStruct((2 * n, d), BF16),
            jax.ShapeDtypeStruct((kv, 2 * n, d), BF16),
        ],
        scratch_shapes=[pltpu.VMEM((2 * n, d), F32)],
        name="prepare",
    )(key_heads.reshape(2 * n, d), value_heads.reshape(2 * n, d), transforms[0])

    arr_a, arr_b = [], []
    for h in range(1, HOPS + 1):
        arr_a.append(shift(buf_a, h))
    rows_blk = pl.BlockSpec((n, None, group, d), lambda g: (0, g, 0, 0))
    own_blk = pl.BlockSpec((None, 2 * n, d), lambda g: (g, 0, 0))
    stat_blk = pl.BlockSpec((None, 8, R), lambda g: (g, 0, 0))
    stats0 = pl.pallas_call(
        functools.partial(near_stats, n=n, d=d, cut=cut, c2=c2),
        grid=(kv,),
        in_specs=[rows_blk, rows_blk, own_blk],
        out_specs=stat_blk,
        out_shape=jax.ShapeDtypeStruct((kv, 8, R), F32),
        cost_estimate=cost(2_500_000_000, 6_000_000),
        name="near_stats",
    )(q4, do4, own)

    buf_b, stats0 = lax.optimization_barrier((buf_b, stats0))
    for h in range(1, HOPS + 1):
        arr_b.append(shift(buf_b, h))

    def call(head, arrived, extra):
        st = pl.BlockSpec((None, 8, R), lambda c, *s: (head, 0, 0))
        turn_spec = pl.BlockSpec((d, d), lambda c, *s: (2 * n // d, 0))
        row_spec = pl.BlockSpec((2 * n, d), lambda c, *s: (0, 0))
        raw = pl.BlockSpec(memory_space=pl.ANY)
        in_specs = [raw, raw] + [row_spec] * HOPS + [turn_spec] * HOPS + [st]
        args = [q4, do4, *arrived, *arr_a, stats0]
        alias = {}
        dms = []
        if head:
            prev_dq, prev_st, prev_dm = extra
            in_specs += [whole(prev_dm.shape)] + [pl.BlockSpec(memory_space=pl.ANY)] * 2
            args += [prev_dm, prev_dq, prev_st]
            alias = {len(args): 0, len(args) + 1: 1}
        else:
            dms = [jax.ShapeDtypeStruct((HOPS, d, d), F32)]
        yshape = jax.ShapeDtypeStruct((2 * n + head * d, d), BF16)
        return pl.pallas_call(
            functools.partial(
                far,
                head=head, n=n, d=d, hops=HOPS, c2=c2, factor=factor, blocks=blocks,
            ),
            grid_spec=pltpu.PrefetchScalarGridSpec(
                num_scalar_prefetch=2,
                grid=(1,),
                in_specs=in_specs,
                out_specs=[pl.BlockSpec((None, d, R), lambda c, *s: (head, 0, 0)), st]
                + [whole(yshape.shape)] * HOPS
                + [whole(x.shape) for x in dms],
                scratch_shapes=[
                    pltpu.VMEM((HOPS, d, d), BF16),
                    pltpu.VMEM((HOPS, n, d), BF16),
                    pltpu.VMEM((HOPS, n, d), BF16),
                    pltpu.VMEM((HOPS, d, n), BF16),
                    pltpu.VMEM((HOPS, n, d), F32),
                    pltpu.VMEM((HOPS, n, d), F32),
                    pltpu.VMEM((HOPS, n, R), F32),
                    pltpu.VMEM((HOPS, n, R), F32),
                    pltpu.VMEM((HOPS, 1, R), F32),
                    pltpu.VMEM((n, group, d), BF16),
                    pltpu.VMEM((n, group, d), BF16),
                    pltpu.SemaphoreType.DMA((2,)),
                ],
            ),
            out_shape=[
                jax.ShapeDtypeStruct((kv, d, R), F32),
                jax.ShapeDtypeStruct((kv, 8, R), F32),
                yshape, yshape, yshape, *dms,
            ],
            input_output_aliases=alias,
            compiler_params=pltpu.CompilerParams(vmem_limit_bytes=48 << 20),
            cost_estimate=cost(9_000_000_000, 6_000_000),
        )(window, first_block, *args)

    dq, st, *ys_a, dm_a = call(0, arr_a, None)
    back_a = []
    for h in range(HOPS):
        back_a.append(shift(ys_a[h], -h - 1))
    dq, st, *ys_b = call(1, arr_b, (dq, st, dm_a))
    back_b = []
    for h, y in enumerate(ys_b):
        back_b.append(shift(y, -h - 1))

    dq_out, own_grad = pl.pallas_call(
        functools.partial(near, n=n, d=d, cut=cut, c2=c2, factor=factor),
        grid=(kv,),
        in_specs=[rows_blk, rows_blk, own_blk, stat_blk, pl.BlockSpec((None, d, R), lambda g: (g, 0, 0))],
        out_specs=[rows_blk, own_blk],
        out_shape=[
            jax.ShapeDtypeStruct((n, kv, group, d), BF16),
            jax.ShapeDtypeStruct((kv, 2 * n, d), F32),
        ],
        cost_estimate=cost(5_000_000_000, 9_000_000),
        name="near",
    )(q4, do4, own, st, dq)

    dt = [b[2 * n :].astype(F32) for b in back_b]
    turn = lax.optimization_barrier(sum(dt[1:], dt[0]))
    peers = lax.axis_size("kv")
    half = turn.astype(BF16)
    total = turn
    for k in range(1, peers):
        sent = lax.ppermute(half, "kv", [(i, (i + k) % peers) for i in range(peers)])
        total = total + sent.astype(F32)

    key_grad, value_grad = pl.pallas_call(
        functools.partial(finish, n=n),
        out_shape=[jax.ShapeDtypeStruct((2 * n, d), BF16)] * 2,
        scratch_shapes=[pltpu.VMEM((2 * n, d), F32)],
        cost_estimate=cost(1_000_000, 3_000_000),
        name="finish",
    )(own_grad, *back_a, *back_b)
    return (
        dq_out.reshape(n, heads, d),
        key_grad.reshape(n, kv, d),
        value_grad.reshape(n, kv, d),
        total[None],
    )


def solution(mesh):
    return jax.shard_map(
        shards,
        mesh=mesh,
        in_specs=(
            P("ctx", "kv", None),
            P("ctx", "kv", None),
            P("ctx", "kv", None),
            P("ctx", "kv", None),
            P("ctx", None, None),
            P("kv"),
            P(),
        ),
        out_specs=(
            P("ctx", "kv", None),
            P("ctx", "kv", None),
            P("ctx", "kv", None),
            P("ctx", None, None),
        ),
        check_vma=False,
    )
```
